32 devices in a mesh: blk: 8 (over z, x), deg: 4 (over y, core).
Axes of the slice: x: 2, y: 2, z: 4, core: 2. Of those that a mesh axis runs over, the one named last changes fastest.
Arguments:
- source: bfloat16 [672, 2048], P('deg', 'blk'), may hold values from -6 to 6
- operators: bfloat16 [12, 672, 672], replicated, may hold values from -0.125 to 0.125
- mie_factor: float32 [672, 2048], P('deg', 'blk'), may hold values from 0.3 to 1.5
- pair_source: int32 [6, 4, 2048], P(None, None, 'blk'), may hold values from 0 to 255
- pair_class: int32 [6, 4, 2048], P(None, None, 'blk'), may hold values from 0 to 11
- pair_scale: bfloat16 [6, 4, 2048], P(None, None, 'blk'), may hold values from 0.25 to 1
Outputs:
- result: float32 [672, 2048], P('deg', 'blk')
The draws below stay inside these ranges and needn't reach their ends.
Inputs may be any that keep to these rules, and one draw needn't show every extreme that they name: `pair_source`: index of a source sphere within the visited block.
All inputs are finite; a program needn't handle non-finite values.
Results may differ from the reference program's by a relative error of at most 0.0075.
Values may be sent and summed in bfloat16 or wider, within the bound.
A program may use at most 64 MiB of HBM per device.

```python
import math
import jax
import jax.numpy as jnp
from jax import lax

COEF = 672
NDIR = 12
PAIRS = 4
STEPS = 6
SPH_DEV = 256
SPHERES = 2048
N_BLK = 8


def place_ends(entries, key, low, high):
    shape = entries.shape
    place = [jax.random.randint(jax.random.fold_in(key, axis), (), 0, shape[axis]) for axis in range(len(shape))]
    entries = entries.at[tuple(place)].set(low)
    longest = shape.index(max(shape))
    place[longest] = (place[longest] + 1) % shape[longest]
    return entries.at[tuple(place)].set(high)


def block_levels(key, dims, shards, low, top_value):
    loudness, own = 1.0, jax.random.fold_in(key, 6)
    for axis_at, shards_of in shards:
        heights = jnp.exp(jax.random.uniform(jax.random.fold_in(own, axis_at), (shards_of,), jnp.float32, low / len(shards), top_value / len(shards)))
        loudness = loudness * jnp.repeat(heights, dims[axis_at] // shards_of).reshape([-1 if axis == axis_at else 1 for axis in range(len(dims))])
    return loudness


def bell_draw(own_key, dims, deviation, most, cuts=(), kind=jnp.bfloat16):
    result = jax.random.normal(own_key, dims, jnp.float32) * deviation
    if len(cuts) > 0:
        result = block_levels(own_key, dims, cuts, -0.22, 0.18) * result
    return jnp.clip(result, min=-most, max=most).astype(kind)


def setup_inputs(seed: int = 0) -> dict:
    key_of = jax.random.split(jax.random.key(seed), 7)
    return {
        "source": bell_draw(key_of[0], (COEF, SPHERES), 1.0, 6.0, ((0, 4), (1, 8))),
        "operators": bell_draw(key_of[1], (NDIR, COEF, COEF), (COEF * PAIRS) ** -0.5, 0.125),
        "mie_factor": jnp.clip(jnp.exp(math.log(1.5) - 1.60943787 * jax.random.uniform(key_of[2], (COEF, SPHERES), jnp.float32) ** block_levels(key_of[2], (COEF, SPHERES), ((0, 4), (1, 8)), -0.2, 0.2)), 0.3, 1.5),
        "pair_source": place_ends(jax.random.randint(key_of[3], (STEPS, PAIRS, SPHERES), 0, SPH_DEV), jax.random.fold_in(key_of[3], 1), 0, SPH_DEV - 1).astype(jnp.int32),
        "pair_class": place_ends(jax.random.randint(key_of[4], (STEPS, PAIRS, SPHERES), 0, NDIR), jax.random.fold_in(key_of[4], 1), 0, NDIR - 1).astype(jnp.int32),
        "pair_scale": jnp.clip(jnp.exp(math.log(1.0) - 1.3862944 * jax.random.uniform(key_of[5], (STEPS, PAIRS, SPHERES), jnp.float32) ** block_levels(key_of[5], (STEPS, PAIRS, SPHERES), ((2, 8),), -0.2, 0.2)), 0.25, 1.0).astype(jnp.bfloat16),
    }


def combine(visiting, indices, kinds, scales, classes):
    picked = jnp.take(visiting, indices, axis=1).astype(jnp.float32)
    onehot = kinds[:, None, :] == jnp.arange(classes, dtype=jnp.int32)[None, :, None]
    weights = jnp.where(onehot, scales[:, None, :], jnp.zeros_like(scales[:, None, :])).astype(jnp.float32)
    gathered = jnp.einsum("rki,kci->cri", picked, weights)
    return gathered.astype(jnp.bfloat16).reshape(classes * visiting.shape[0], visiting.shape[1])


def reference(source, operators, mie_factor, pair_source, pair_class, pair_scale):
    blocks = source.reshape(COEF, N_BLK, SPH_DEV)
    weight_flat = jnp.transpose(operators, (1, 0, 2)).reshape(COEF, NDIR * COEF)

    def one_block(block_index):
        target_field = jnp.zeros((COEF, SPH_DEV), jnp.float32)
        offset_start = (block_index * SPH_DEV).astype(jnp.int32)
        for cycle_step in range(STEPS):
            anchor = ((block_index - cycle_step) % N_BLK).astype(jnp.int32)
            visiting = lax.dynamic_index_in_dim(blocks, anchor, 1, keepdims=False)
            indices = lax.dynamic_slice_in_dim(pair_source[cycle_step], offset_start, SPH_DEV, 1)
            kinds = lax.dynamic_slice_in_dim(pair_class[cycle_step], offset_start, SPH_DEV, 1)
            scales = lax.dynamic_slice_in_dim(pair_scale[cycle_step], offset_start, SPH_DEV, 1)
            combined = combine(visiting, indices, kinds, scales, NDIR)
            target_field = target_field + jnp.dot(weight_flat, combined, preferred_element_type=jnp.float32)
        return target_field

    fields = lax.map(one_block, jnp.arange(N_BLK, dtype=jnp.int32))
    target_field = jnp.transpose(fields, (1, 0, 2)).reshape(COEF, SPHERES)
    return source.astype(jnp.float32) - mie_factor * target_field
```

```python
import functools

import jax
import jax.numpy as jnp
from jax import lax
from jax.experimental import pallas as pl
from jax.experimental.pallas import tpu as pltpu
from jax.sharding import PartitionSpec as P

MESH = pl.DeviceIdType.MESH
LANES = 128


def window_of(rows, full, n_deg):
    lows = [position * rows // LANES * LANES for position in range(n_deg)]
    ends = [(position + 1) * rows - low for position, low in enumerate(lows)]
    main = min(-(-max(ends) // LANES) * LANES, full - lows[-1]) // LANES * LANES
    tail = full - lows[-1] - main
    assert max(ends[:-1]) <= main and 0 <= tail < LANES
    return main, tail


def kernel(
    n_blk,
    n_deg,
    source_ref,
    op_ref,
    mie_ref,
    index_ref,
    kind_ref,
    scale_ref,
    out_ref,
    visit,
    hot,
    acc,
    total,
    weights,
    send_buf,
    recv_buf,
    visit_send,
    visit_recv,
    field_send,
    field_recv,
    op_sem,
):
    rows, spheres = source_ref.shape
    classes, full, _ = op_ref.shape
    steps, slots, _ = index_ref.shape
    group = weights.shape[2] // rows
    n_groups = n_deg // group
    blk = lax.axis_index("blk")
    deg = lax.axis_index("deg")
    mine = deg // group

    main, tail = window_of(rows, full, n_deg)

    def op_copy(part):
        return pltpu.make_async_copy(
            op_ref.at[:, pl.ds(part * group * rows, group * rows), :],
            weights.at[part],
            op_sem.at[part],
        )

    for part in range(n_groups):
        op_copy(part).start()

    def partner(shift):
        inner = lax.rem(lax.rem(deg, group) + shift % group, group)
        outer = lax.rem(mine + shift // group, n_groups)
        return outer * group + inner

    barrier = pltpu.get_barrier_semaphore()
    for step in range(1, steps):
        pl.semaphore_signal(
            barrier, inc=1, device_id=(lax.rem(blk + n_blk - step, n_blk), deg), device_id_type=MESH
        )
    for shift in range(1, n_deg):
        pl.semaphore_signal(
            barrier, inc=1, device_id=(blk, lax.rem(deg + shift, n_deg)), device_id_type=MESH
        )
    pl.semaphore_wait(barrier, steps - 1 + n_deg - 1)

    def visit_copy(step):
        return pltpu.make_async_remote_copy(
            src_ref=source_ref,
            dst_ref=visit.at[step],
            send_sem=visit_send.at[step],
            recv_sem=visit_recv.at[step],
            device_id=(lax.rem(blk + step, n_blk), deg),
            device_id_type=MESH,
        )

    for step in range(1, steps):
        visit_copy(step).start()

    visit[0] = source_ref[...]
    acc[...] = jnp.zeros(acc.shape, acc.dtype)
    shift_rows = pl.multiple_of(lax.rem(deg * rows, LANES), 8)

    def one_visit(step, carry):
        sphere = lax.broadcasted_iota(jnp.int32, (spheres, spheres), 0)
        for slot in range(slots):
            row = index_ref[step, slot : slot + 1, :]
            hit = jnp.where(sphere == row, 1.0, 0.0).astype(jnp.bfloat16)
            hot[slot] = hit.reshape(hot.shape[1:])
        kinds = kind_ref[step]
        scales = scale_ref[step].astype(jnp.float32)

        @pl.when(step > 0)
        def _():
            visit_copy(step).wait_recv()

        value = visit[step]
        for kind in range(classes):
            weight = jnp.where(kinds == kind, scales, 0.0)
            table = None
            for slot in range(slots):
                line = jnp.broadcast_to(weight[slot : slot + 1, :], (16, spheres))
                term = hot[slot] * line.astype(jnp.bfloat16)[None]
                table = term if table is None else table + term
            part = jnp.dot(
                value, table.reshape(spheres, spheres), preferred_element_type=jnp.float32
            )
            acc[kind, pl.ds(shift_rows, rows), :] += part
        return carry

    lax.fori_loop(0, steps, one_visit, 0)

    for part in range(n_groups):
        op_copy(part).wait()
    low = pl.multiple_of(deg * rows // LANES * LANES, LANES)

    def field_copy(shift):
        target = partner(shift)
        return pltpu.make_async_remote_copy(
            src_ref=send_buf.at[shift],
            dst_ref=recv_buf.at[shift],
            send_sem=field_send.at[shift],
            recv_sem=field_recv.at[shift],
            device_id=(blk, target),
            device_id_type=MESH,
        )

    own = None
    for outer in list(range(1, n_groups)) + [0]:
        which = lax.rem(mine + outer, n_groups)
        field = None
        for kind in range(classes):
            term = jnp.dot(
                weights[which, kind, :, pl.ds(low, main)],
                acc[kind, :main, :].astype(jnp.bfloat16),
                preferred_element_type=jnp.float32,
            )
            if tail:
                term += jnp.dot(
                    weights[which, kind, :, full - tail :],
                    acc[kind, main:, :].astype(jnp.bfloat16),
                    preferred_element_type=jnp.float32,
                )
            field = term if field is None else field + term
        total[...] = field
        for inner in list(range(1, group)) + [0]:
            shift = outer * group + inner
            place = lax.rem(lax.rem(deg, group) + inner, group)
            piece = total[pl.ds(pl.multiple_of(place * rows, 8), rows), :]
            if shift == 0:
                own = piece
            else:
                send_buf[shift] = piece.astype(jnp.bfloat16)
                field_copy(shift).start()

    for shift in list(range(1, group)) + list(range(group, n_deg)):
        field_copy(shift).wait_recv()
        own = own + recv_buf[shift].astype(jnp.float32)
    out_ref[...] = source_ref[...].astype(jnp.float32) - mie_ref[...] * own
    for step in range(1, steps):
        visit_copy(step).wait_send()
    for shift in range(1, n_deg):
        field_copy(shift).wait_send()


def solution(mesh):
    n_blk = mesh.shape["blk"]
    n_deg = mesh.shape["deg"]

    def local(source, operators, mie_factor, pair_source, pair_class, pair_scale):
        rows, spheres = source.shape
        classes, full, _ = operators.shape
        steps, slots, _ = pair_source.shape
        group = 2 if n_deg % 2 == 0 else 1
        main, tail = window_of(rows, full, n_deg)
        vmem = pl.BlockSpec(memory_space=pltpu.VMEM)
        return pl.pallas_call(
            functools.partial(kernel, n_blk, n_deg),
            out_shape=jax.ShapeDtypeStruct((rows, spheres), jnp.float32),
            in_specs=[vmem, pl.BlockSpec(memory_space=pltpu.HBM), vmem, vmem, vmem, vmem],
            out_specs=vmem,
            scratch_shapes=[
                pltpu.VMEM((steps, rows, spheres), jnp.bfloat16),
                pltpu.VMEM((slots, spheres // 16, 16, spheres), jnp.bfloat16),
                pltpu.VMEM((classes, main + tail, spheres), jnp.float32),
                pltpu.VMEM((group * rows, spheres), jnp.float32),
                pltpu.VMEM((n_deg // group, classes, group * rows, full), jnp.bfloat16),
                pltpu.VMEM((n_deg, rows, spheres), jnp.bfloat16),
                pltpu.VMEM((n_deg, rows, spheres), jnp.bfloat16),
                pltpu.SemaphoreType.DMA((steps,)),
                pltpu.SemaphoreType.DMA((steps,)),
                pltpu.SemaphoreType.DMA((n_deg,)),
                pltpu.SemaphoreType.DMA((n_deg,)),
                pltpu.SemaphoreType.DMA((n_deg // group,)),
            ],
            compiler_params=pltpu.CompilerParams(
                collective_id=0, has_side_effects=True, vmem_limit_bytes=56 * 1024 * 1024
            ),
        )(source, operators, mie_factor, pair_source, pair_class, pair_scale)

    return jax.shard_map(
        local,
        mesh=mesh,
        in_specs=(
            P("deg", "blk"),
            P(),
            P("deg", "blk"),
            P(None, None, "blk"),
            P(None, None, "blk"),
            P(None, None, "blk"),
        ),
        out_specs=P("deg", "blk"),
        check_vma=False,
    )
```

```python
import functools

import jax
import jax.numpy as jnp
from jax import lax
from jax.experimental import pallas as pl
from jax.experimental.pallas import tpu as pltpu
from jax.sharding import PartitionSpec as P

MESH = pl.DeviceIdType.MESH
LANES = 128
PIECES = 2


def window_of(rows, full, n_deg):
    lows = [position * rows // LANES * LANES for position in range(n_deg)]
    ends = [(position + 1) * rows - low for position, low in enumerate(lows)]
    main = min(-(-max(ends) // LANES) * LANES, full - lows[-1]) // LANES * LANES
    tail = full - lows[-1] - main
    assert max(ends[:-1]) <= main and 0 <= tail < LANES
    return main, tail


def kernel(
    n_blk,
    n_deg,
    source_ref,
    op_ref,
    mie_ref,
    index_ref,
    kind_ref,
    scale_ref,
    out_ref,
    visit,
    hot,
    acc,
    total,
    weights,
    send_buf,
    recv_buf,
    visit_send,
    visit_recv,
    field_send,
    field_recv,
    op_sem,
):
    rows, spheres = source_ref.shape
    classes, full, _ = op_ref.shape
    steps, slots, _ = index_ref.shape
    group = weights.shape[2] // rows
    n_groups = n_deg // group
    blk = lax.axis_index("blk")
    deg = lax.axis_index("deg")
    mine = deg // group

    main, tail = window_of(rows, full, n_deg)

    def op_copy(part):
        return pltpu.make_async_copy(
            op_ref.at[:, pl.ds(part * group * rows, group * rows), :],
            weights.at[part],
            op_sem.at[part],
        )

    for part in range(n_groups):
        op_copy(part).start()

    def partner(shift):
        inner = lax.rem(lax.rem(deg, group) + shift % group, group)
        outer = lax.rem(mine + shift // group, n_groups)
        return outer * group + inner

    side = lax.rem(blk, 2)
    ahead = (steps - 1) // 2
    first_slot = 1 + side * (steps - 2)

    def to_blk(shift):
        return (lax.rem(blk + shift + n_blk, n_blk), deg)

    barrier = pltpu.get_barrier_semaphore()
    for source_of in (-2, 1 - 2 * side, side * (steps - 2) - (steps - 1)):
        pl.semaphore_signal(barrier, inc=1, device_id=to_blk(source_of), device_id_type=MESH)
    for shift in range(1, n_deg):
        pl.semaphore_signal(
            barrier, inc=1, device_id=(blk, lax.rem(deg + shift, n_deg)), device_id_type=MESH
        )
    pl.semaphore_wait(barrier, 3 + n_deg - 1)

    def move(src, slot, target, kind):
        copies = []
        width = spheres // PIECES
        for piece in range(PIECES):
            lanes = pl.ds(piece * width, width)
            copies.append(
                pltpu.make_async_remote_copy(
                    src_ref=src.at[:, lanes],
                    dst_ref=visit.at[slot, :, lanes],
                    send_sem=visit_send.at[kind, piece],
                    recv_sem=visit_recv.at[slot, piece],
                    device_id=to_blk(target),
                    device_id_type=MESH,
                )
            )
        return copies

    def direct():
        return move(source_ref, first_slot, first_slot, 0)

    def along(hop, src):
        return move(src, 2 * hop, 2, hop)

    def across(hop):
        return move(visit.at[2 * hop], 2 * hop + 1 - 2 * side, 1 - 2 * side, ahead + hop)

    for copy in along(1, source_ref) + direct():
        copy.start()

    visit[0] = source_ref[...]
    acc[...] = jnp.zeros(acc.shape, acc.dtype)
    shift_rows = pl.multiple_of(lax.rem(deg * rows, LANES), 8)

    def one_visit(step):
        sphere = lax.broadcasted_iota(jnp.int32, (spheres, spheres), 0)
        for slot in range(slots):
            row = index_ref[step, slot : slot + 1, :]
            hit = jnp.where(sphere == row, 1.0, 0.0).astype(jnp.bfloat16)
            hot[slot] = hit.reshape(hot.shape[1:])
        kinds = kind_ref[step]
        scales = scale_ref[step].astype(jnp.float32)
        value = visit[step]
        for kind in range(classes):
            weight = jnp.where(kinds == kind, scales, 0.0)
            table = None
            for slot in range(slots):
                line = jnp.broadcast_to(weight[slot : slot + 1, :], (16, spheres))
                term = hot[slot] * line.astype(jnp.bfloat16)[None]
                table = term if table is None else table + term
            part = jnp.dot(
                value, table.reshape(spheres, spheres), preferred_element_type=jnp.float32
            )
            acc[kind, pl.ds(shift_rows, rows), :] += part

    def two_visits(turn, carry):
        one_visit(2 * turn)

        @pl.when(turn < ahead)
        def _():
            arrived = move(source_ref, 2 * turn + 2, 2, 0)
            onward = along(turn + 2, visit.at[2 * turn + 2])
            over = across(turn + 1)
            for piece in range(PIECES):
                arrived[piece].wait_recv()

                @pl.when(turn + 1 < ahead)
                def _():
                    onward[piece].start()

                over[piece].start()

        odd = lax.rem(2 * turn - 1 + 2 * side + steps, steps)
        for copy in move(source_ref, odd, 2, 0):
            copy.wait_recv()
        one_visit(odd)
        return carry

    lax.fori_loop(0, steps // 2, two_visits, 0)

    for part in range(n_groups):
        op_copy(part).wait()
    low = pl.multiple_of(deg * rows // LANES * LANES, LANES)

    def field_copy(shift):
        target = partner(shift)
        return pltpu.make_async_remote_copy(
            src_ref=send_buf.at[shift],
            dst_ref=recv_buf.at[shift],
            send_sem=field_send.at[shift],
            recv_sem=field_recv.at[shift],
            device_id=(blk, target),
            device_id_type=MESH,
        )

    own = None
    for outer in list(range(1, n_groups)) + [0]:
        which = lax.rem(mine + outer, n_groups)
        field = None
        for kind in range(classes):
            term = jnp.dot(
                weights[which, kind, :, pl.ds(low, main)],
                acc[kind, :main, :].astype(jnp.bfloat16),
                preferred_element_type=jnp.float32,
            )
            if tail:
                term += jnp.dot(
                    weights[which, kind, :, full - tail :],
                    acc[kind, main:, :].astype(jnp.bfloat16),
                    preferred_element_type=jnp.float32,
                )
            field = term if field is None else field + term
        total[...] = field
        for inner in list(range(1, group)) + [0]:
            shift = outer * group + inner
            place = lax.rem(lax.rem(deg, group) + inner, group)
            piece = total[pl.ds(pl.multiple_of(place * rows, 8), rows), :]
            if shift == 0:
                own = piece
            else:
                send_buf[shift] = piece.astype(jnp.bfloat16)
                field_copy(shift).start()

    for shift in list(range(1, group)) + list(range(group, n_deg)):
        field_copy(shift).wait_recv()
        own = own + recv_buf[shift].astype(jnp.float32)
    out_ref[...] = source_ref[...].astype(jnp.float32) - mie_ref[...] * own
    sent = direct()
    for hop in range(1, ahead + 1):
        sent += along(hop, source_ref) + across(hop)
    for copy in sent:
        copy.wait_send()
    for shift in range(1, n_deg):
        field_copy(shift).wait_send()


def solution(mesh):
    n_blk = mesh.shape["blk"]
    n_deg = mesh.shape["deg"]

    def local(source, operators, mie_factor, pair_source, pair_class, pair_scale):
        rows, spheres = source.shape
        classes, full, _ = operators.shape
        steps, slots, _ = pair_source.shape
        group = 2 if n_deg % 2 == 0 else 1
        main, tail = window_of(rows, full, n_deg)
        vmem = pl.BlockSpec(memory_space=pltpu.VMEM)
        return pl.pallas_call(
            functools.partial(kernel, n_blk, n_deg),
            out_shape=jax.ShapeDtypeStruct((rows, spheres), jnp.float32),
            in_specs=[vmem, pl.BlockSpec(memory_space=pltpu.HBM), vmem, vmem, vmem, vmem],
            out_specs=vmem,
            scratch_shapes=[
                pltpu.VMEM((steps, rows, spheres), jnp.bfloat16),
                pltpu.VMEM((slots, spheres // 16, 16, spheres), jnp.bfloat16),
                pltpu.VMEM((classes, main + tail, spheres), jnp.float32),
                pltpu.VMEM((group * rows, spheres), jnp.float32),
                pltpu.VMEM((n_deg // group, classes, group * rows, full), jnp.bfloat16),
                pltpu.VMEM((n_deg, rows, spheres), jnp.bfloat16),
                pltpu.VMEM((n_deg, rows, spheres), jnp.bfloat16),
                pltpu.SemaphoreType.DMA((2 * ((steps - 1) // 2) + 1, PIECES)),
                pltpu.SemaphoreType.DMA((steps, PIECES)),
                pltpu.SemaphoreType.DMA((n_deg,)),
                pltpu.SemaphoreType.DMA((n_deg,)),
                pltpu.SemaphoreType.DMA((n_deg // group,)),
            ],
            compiler_params=pltpu.CompilerParams(
                collective_id=0, has_side_effects=True, vmem_limit_bytes=56 * 1024 * 1024
            ),
        )(source, operators, mie_factor, pair_source, pair_class, pair_scale)

    return jax.shard_map(
        local,
        mesh=mesh,
        in_specs=(
            P("deg", "blk"),
            P(),
            P("deg", "blk"),
            P(None, None, "blk"),
            P(None, None, "blk"),
            P(None, None, "blk"),
        ),
        out_specs=P("deg", "blk"),
        check_vma=False,
    )
```

```python
import functools

import jax
import jax.numpy as jnp
from jax import lax
from jax.experimental import pallas as pl
from jax.experimental.pallas import tpu as pltpu
from jax.sharding import PartitionSpec as P

MESH = pl.DeviceIdType.MESH
LANES = 128
PIECES = 3


def window_of(rows, full, n_deg):
    lows = [position * rows // LANES * LANES for position in range(n_deg)]
    ends = [(position + 1) * rows - low for position, low in enumerate(lows)]
    main = min(-(-max(ends) // LANES) * LANES, full - lows[-1]) // LANES * LANES
    tail = full - lows[-1] - main
    assert max(ends[:-1]) <= main and 0 <= tail < LANES
    return main, tail


def pieces_of(rows):
    return next(count for count in (PIECES, 2, 1) if rows % (8 * count) == 0)


def kernel(
    n_blk,
    n_deg,
    source_ref,
    op_ref,
    mie_hbm,
    index_hbm,
    kind_hbm,
    scale_hbm,
    out_ref,
    mie_ref,
    index_ref,
    kind_ref,
    scale_ref,
    in_sem,
    visit,
    hot,
    acc,
    total,
    weights,
    send_buf,
    recv_buf,
    visit_send,
    visit_recv,
    field_send,
    field_recv,
    op_sem,
):
    rows, spheres = source_ref.shape
    classes, full, _ = op_ref.shape
    steps, slots, _ = index_ref.shape
    group = weights.shape[2] // rows
    n_groups = n_deg // group
    blk = lax.axis_index("blk")
    deg = lax.axis_index("deg")
    mine = deg // group

    main, tail = window_of(rows, full, n_deg)

    fetches = [
        pltpu.make_async_copy(src, dst, in_sem.at[which])
        for which, (src, dst) in enumerate(
            (
                (source_ref, visit.at[0]),
                (index_hbm, index_ref),
                (kind_hbm, kind_ref),
                (scale_hbm, scale_ref),
                (mie_hbm, mie_ref),
            )
        )
    ]
    for fetch in fetches:
        fetch.start()

    def op_copy(part):
        return pltpu.make_async_copy(
            op_ref.at[:, pl.ds(part * group * rows, group * rows), :],
            weights.at[part],
            op_sem.at[part],
        )


    def partner(shift):
        inner = lax.rem(lax.rem(deg, group) + shift % group, group)
        outer = lax.rem(mine + shift // group, n_groups)
        return outer * group + inner

    side = lax.rem(blk, 2)
    ahead = (steps - 1) // 2
    pieces = pieces_of(rows)
    first_slot = 1 + side * (steps - 2)

    def to_blk(shift):
        return (lax.rem(blk + shift + n_blk, n_blk), deg)

    barrier = pltpu.get_barrier_semaphore()
    for source_of in (-2, 1 - 2 * side, side * (steps - 2) - (steps - 1)):
        pl.semaphore_signal(barrier, inc=1, device_id=to_blk(source_of), device_id_type=MESH)
    for shift in range(1, n_deg):
        pl.semaphore_signal(
            barrier, inc=1, device_id=(blk, lax.rem(deg + shift, n_deg)), device_id_type=MESH
        )
    pl.semaphore_wait(barrier, 3 + n_deg - 1)

    def move(src, slot, target, kind):
        copies = []
        height = rows // pieces
        for piece in range(pieces):
            part = pl.ds(piece * height, height)
            copies.append(
                pltpu.make_async_remote_copy(
                    src_ref=src.at[part],
                    dst_ref=visit.at[slot, part],
                    send_sem=visit_send.at[kind, piece],
                    recv_sem=visit_recv.at[slot, piece],
                    device_id=to_blk(target),
                    device_id_type=MESH,
                )
            )
        return copies

    def direct():
        return move(source_ref, first_slot, first_slot, 0)

    def along(hop, src):
        return move(src, 2 * hop, 2, hop)

    def across(hop):
        return move(visit.at[2 * hop], 2 * hop + 1 - 2 * side, 1 - 2 * side, ahead + hop)

    for copy in along(1, source_ref) + direct():
        copy.start()
    for part in range(n_groups):
        op_copy(part).start()

    acc[...] = jnp.zeros(acc.shape, acc.dtype)
    shift_rows = pl.multiple_of(lax.rem(deg * rows, LANES), 8)

    def one_visit(step):
        sphere = lax.broadcasted_iota(jnp.int32, (spheres, spheres), 0)
        for slot in range(slots):
            row = index_ref[step, slot : slot + 1, :]
            hit = jnp.where(sphere == row, 1.0, 0.0).astype(jnp.bfloat16)
            hot[slot] = hit.reshape(hot.shape[1:])
        kinds = kind_ref[step]
        scales = scale_ref[step].astype(jnp.float32)
        value = visit[step]
        for kind in range(classes):
            weight = jnp.where(kinds == kind, scales, 0.0)
            table = None
            for slot in range(slots):
                line = jnp.broadcast_to(weight[slot : slot + 1, :], (16, spheres))
                term = hot[slot] * line.astype(jnp.bfloat16)[None]
                table = term if table is None else table + term
            part = jnp.dot(
                value, table.reshape(spheres, spheres), preferred_element_type=jnp.float32
            )
            acc[kind, pl.ds(shift_rows, rows), :] += part

    def take_turn(turn, carry):
        last = 2 * ahead + 1
        even = lax.rem(turn, 2) * (1 - turn // last)
        behind = (turn - 1 + steps) // 2 - steps // 2
        odd = lax.rem(2 * behind - 1 + 2 * side + 2 * steps, steps)
        moved = (turn + last - 1) // last
        step = moved * (even * (turn + 1) + (1 - even) * odd)

        @pl.when(even == 1)
        def _():
            hop = (turn + 1) // 2
            arrived = move(source_ref, 2 * hop, 2, 0)
            onward = along(hop + 1, visit.at[2 * hop])
            over = across(hop)
            for piece in range(pieces):
                arrived[piece].wait_recv()

                @pl.when(hop < ahead)
                def _():
                    onward[piece].start()

                over[piece].start()

        @pl.when(moved * (1 - even) == 1)
        def _():
            for copy in move(source_ref, odd, 2, 0):
                copy.wait_recv()

        one_visit(step)
        return carry

    for fetch in fetches:
        fetch.wait()
    lax.fori_loop(0, steps, take_turn, 0)

    for part in range(n_groups):
        op_copy(part).wait()
    low = pl.multiple_of(deg * rows // LANES * LANES, LANES)

    def field_copy(shift):
        target = partner(shift)
        return pltpu.make_async_remote_copy(
            src_ref=send_buf.at[shift],
            dst_ref=recv_buf.at[shift],
            send_sem=field_send.at[shift],
            recv_sem=field_recv.at[shift],
            device_id=(blk, target),
            device_id_type=MESH,
        )

    own = None
    for outer in list(range(1, n_groups)) + [0]:
        which = lax.rem(mine + outer, n_groups)
        field = None
        for kind in range(classes):
            term = jnp.dot(
                weights[which, kind, :, pl.ds(low, main)],
                acc[kind, :main, :].astype(jnp.bfloat16),
                preferred_element_type=jnp.float32,
            )
            if tail:
                term += jnp.dot(
                    weights[which, kind, :, full - tail :],
                    acc[kind, main:, :].astype(jnp.bfloat16),
                    preferred_element_type=jnp.float32,
                )
            field = term if field is None else field + term
        total[...] = field
        for inner in list(range(1, group)) + [0]:
            shift = outer * group + inner
            place = lax.rem(lax.rem(deg, group) + inner, group)
            piece = total[pl.ds(pl.multiple_of(place * rows, 8), rows), :]
            if shift == 0:
                own = piece
            else:
                send_buf[shift] = piece.astype(jnp.bfloat16)
                field_copy(shift).start()

    for shift in list(range(1, group)) + list(range(group, n_deg)):
        field_copy(shift).wait_recv()
        own = own + recv_buf[shift].astype(jnp.float32)
    out_ref[...] = visit[0].astype(jnp.float32) - mie_ref[...] * own
    sent = direct()
    for hop in range(1, ahead + 1):
        sent += along(hop, source_ref) + across(hop)
    for copy in sent:
        copy.wait_send()
    for shift in range(1, n_deg):
        field_copy(shift).wait_send()


def solution(mesh):
    n_blk = mesh.shape["blk"]
    n_deg = mesh.shape["deg"]

    def local(source, operators, mie_factor, pair_source, pair_class, pair_scale):
        rows, spheres = source.shape
        classes, full, _ = operators.shape
        steps, slots, _ = pair_source.shape
        group = 2 if n_deg % 2 == 0 else 1
        main, tail = window_of(rows, full, n_deg)
        vmem = pl.BlockSpec(memory_space=pltpu.VMEM)
        return pl.pallas_call(
            functools.partial(kernel, n_blk, n_deg),
            out_shape=jax.ShapeDtypeStruct((rows, spheres), jnp.float32),
            in_specs=[pl.BlockSpec(memory_space=pltpu.HBM)] * 6,
            out_specs=vmem,
            scratch_shapes=[
                pltpu.VMEM((rows, spheres), jnp.float32),
                pltpu.VMEM(pair_source.shape, pair_source.dtype),
                pltpu.VMEM(pair_class.shape, pair_class.dtype),
                pltpu.VMEM(pair_scale.shape, pair_scale.dtype),
                pltpu.SemaphoreType.DMA((5,)),
                pltpu.VMEM((steps, rows, spheres), jnp.bfloat16),
                pltpu.VMEM((slots, spheres // 16, 16, spheres), jnp.bfloat16),
                pltpu.VMEM((classes, main + tail, spheres), jnp.float32),
                pltpu.VMEM((group * rows, spheres), jnp.float32),
                pltpu.VMEM((n_deg // group, classes, group * rows, full), jnp.bfloat16),
                pltpu.VMEM((n_deg, rows, spheres), jnp.bfloat16),
                pltpu.VMEM((n_deg, rows, spheres), jnp.bfloat16),
                pltpu.SemaphoreType.DMA((2 * ((steps - 1) // 2) + 1, pieces_of(rows))),
                pltpu.SemaphoreType.DMA((steps, pieces_of(rows))),
                pltpu.SemaphoreType.DMA((n_deg,)),
                pltpu.SemaphoreType.DMA((n_deg,)),
                pltpu.SemaphoreType.DMA((n_deg // group,)),
            ],
            compiler_params=pltpu.CompilerParams(
                collective_id=0, has_side_effects=True, vmem_limit_bytes=56 * 1024 * 1024
            ),
        )(source, operators, mie_factor, pair_source, pair_class, pair_scale)

    return jax.shard_map(
        local,
        mesh=mesh,
        in_specs=(
            P("deg", "blk"),
            P(),
            P("deg", "blk"),
            P(None, None, "blk"),
            P(None, None, "blk"),
            P(None, None, "blk"),
        ),
        out_specs=P("deg", "blk"),
        check_vma=False,
    )
```

```python
import functools

import jax
import jax.numpy as jnp
from jax import lax
from jax.experimental import pallas as pl
from jax.experimental.pallas import tpu as pltpu
from jax.sharding import PartitionSpec as P

MESH = pl.DeviceIdType.MESH
LANES = 128
PIECES = 3


def window_of(rows, full, n_deg):
    lows = [position * rows // LANES * LANES for position in range(n_deg)]
    ends = [(position + 1) * rows - low for position, low in enumerate(lows)]
    main = min(-(-max(ends) // LANES) * LANES, full - lows[-1]) // LANES * LANES
    tail = full - lows[-1] - main
    assert max(ends[:-1]) <= main and 0 <= tail < LANES
    return main, tail


def pieces_of(rows):
    return next(count for count in (PIECES, 2, 1) if rows % (8 * count) == 0)


def kernel(
    n_blk,
    n_deg,
    source_ref,
    op_ref,
    mie_hbm,
    index_hbm,
    kind_hbm,
    scale_hbm,
    out_ref,
    mie_ref,
    index_ref,
    kind_ref,
    scale_ref,
    in_sem,
    visit,
    hot,
    acc,
    weights,
    send_buf,
    recv_buf,
    visit_send,
    visit_recv,
    field_send,
    field_recv,
    op_sem,
):
    rows, spheres = source_ref.shape
    classes, full, _ = op_ref.shape
    steps, slots, _ = index_ref.shape
    group = 2 if n_deg % 2 == 0 else 1
    n_groups = n_deg // group
    blk = lax.axis_index("blk")
    deg = lax.axis_index("deg")
    mine = deg // group

    main, tail = window_of(rows, full, n_deg)

    fetches = [
        pltpu.make_async_copy(src, dst, in_sem.at[which])
        for which, (src, dst) in enumerate(
            (
                (source_ref, visit.at[0]),
                (index_hbm, index_ref),
                (kind_hbm, kind_ref),
                (scale_hbm, scale_ref),
                (mie_hbm, mie_ref),
            )
        )
    ]
    for fetch in fetches:
        fetch.start()

    def op_copy(part):
        return pltpu.make_async_copy(
            op_ref.at[:, pl.ds(part * rows, rows), :],
            weights.at[part],
            op_sem.at[part],
        )


    side = lax.rem(blk, 2)
    ahead = (steps - 1) // 2
    pieces = pieces_of(rows)
    first_slot = 1 + side * (steps - 2)

    def to_blk(shift):
        return (lax.rem(blk + shift + n_blk, n_blk), deg)

    barrier = pltpu.get_barrier_semaphore()
    for source_of in (-2, 1 - 2 * side, side * (steps - 2) - (steps - 1)):
        pl.semaphore_signal(barrier, inc=1, device_id=to_blk(source_of), device_id_type=MESH)
    for shift in range(1, n_deg):
        pl.semaphore_signal(
            barrier, inc=1, device_id=(blk, lax.rem(deg + shift, n_deg)), device_id_type=MESH
        )
    pl.semaphore_wait(barrier, 3 + n_deg - 1)

    def move(src, slot, target, kind):
        copies = []
        height = rows // pieces
        for piece in range(pieces):
            part = pl.ds(piece * height, height)
            copies.append(
                pltpu.make_async_remote_copy(
                    src_ref=src.at[part],
                    dst_ref=visit.at[slot, part],
                    send_sem=visit_send.at[kind, piece],
                    recv_sem=visit_recv.at[slot, piece],
                    device_id=to_blk(target),
                    device_id_type=MESH,
                )
            )
        return copies

    def direct():
        return move(source_ref, first_slot, first_slot, 0)

    def along(hop, src):
        return move(src, 2 * hop, 2, hop)

    def across(hop):
        return move(visit.at[2 * hop], 2 * hop + 1 - 2 * side, 1 - 2 * side, ahead + hop)

    for copy in along(1, source_ref) + direct():
        copy.start()
    for part in range(n_deg):
        op_copy(part).start()

    acc[...] = jnp.zeros(acc.shape, acc.dtype)
    shift_rows = pl.multiple_of(lax.rem(deg * rows, LANES), 8)

    def one_visit(step):
        sphere = lax.broadcasted_iota(jnp.int32, (spheres, spheres), 0)
        for slot in range(slots):
            row = index_ref[step, slot : slot + 1, :]
            hit = jnp.where(sphere == row, 1.0, 0.0).astype(jnp.bfloat16)
            hot[slot] = hit.reshape(hot.shape[1:])
        kinds = kind_ref[step]
        scales = scale_ref[step].astype(jnp.float32)
        value = visit[step]
        for kind in range(classes):
            weight = jnp.where(kinds == kind, scales, 0.0)
            table = None
            for slot in range(slots):
                line = jnp.broadcast_to(weight[slot : slot + 1, :], (16, spheres))
                term = hot[slot] * line.astype(jnp.bfloat16)[None]
                table = term if table is None else table + term
            part = jnp.dot(
                value, table.reshape(spheres, spheres), preferred_element_type=jnp.float32
            )
            acc[kind, pl.ds(shift_rows, rows), :] += part

    def take_turn(turn, carry):
        last = 2 * ahead + 1
        even = lax.rem(turn, 2) * (1 - turn // last)
        behind = (turn - 1 + steps) // 2 - steps // 2
        odd = lax.rem(2 * behind - 1 + 2 * side + 2 * steps, steps)
        moved = (turn + last - 1) // last
        step = moved * (even * (turn + 1) + (1 - even) * odd)

        @pl.when(even == 1)
        def _():
            hop = (turn + 1) // 2
            arrived = move(source_ref, 2 * hop, 2, 0)
            onward = along(hop + 1, visit.at[2 * hop])
            over = across(hop)
            for piece in range(pieces):
                arrived[piece].wait_recv()

                @pl.when(hop < ahead)
                def _():
                    onward[piece].start()

                over[piece].start()

        @pl.when(moved * (1 - even) == 1)
        def _():
            for copy in move(source_ref, odd, 2, 0):
                copy.wait_recv()

        one_visit(step)
        return carry

    for fetch in fetches:
        fetch.wait()
    lax.fori_loop(0, steps, take_turn, 0)

    for part in range(n_deg):
        op_copy(part).wait()
    low = pl.multiple_of(deg * rows // LANES * LANES, LANES)

    core = lax.rem(deg, group)

    def field_copy(slot, target):
        return pltpu.make_async_remote_copy(
            src_ref=send_buf.at[slot],
            dst_ref=recv_buf.at[slot],
            send_sem=field_send.at[slot],
            recv_sem=field_recv.at[slot],
            device_id=(blk, target),
            device_id_type=MESH,
        )

    def to_pair(outer):
        return field_copy(outer, mine * group + lax.rem(core + 1, group))

    def to_far(outer):
        return field_copy(n_groups + outer, lax.rem(mine + outer, n_groups) * group + core)

    def field_of(owner):
        field = None
        for kind in range(classes):
            term = jnp.dot(
                weights[owner, kind, :, pl.ds(low, main)],
                acc[kind, :main, :].astype(jnp.bfloat16),
                preferred_element_type=jnp.float32,
            )
            if tail:
                term += jnp.dot(
                    weights[owner, kind, :, full - tail :],
                    acc[kind, main:, :].astype(jnp.bfloat16),
                    preferred_element_type=jnp.float32,
                )
            field = term if field is None else field + term
        return field

    started = []
    for outer in list(range(1, n_groups)) + [0]:
        first = lax.rem(mine + outer, n_groups) * group
        if group > 1:
            send_buf[outer] = field_of(first + lax.rem(core + 1, group)).astype(jnp.bfloat16)
            to_pair(outer).start()
            started.append(to_pair(outer))
        own = field_of(first + core)
        if group > 1:
            to_pair(outer).wait_recv()
            own = own + recv_buf[outer].astype(jnp.float32)
        if outer > 0:
            send_buf[n_groups + outer] = own.astype(jnp.bfloat16)
            to_far(outer).start()
            started.append(to_far(outer))

    for outer in range(1, n_groups):
        to_far(outer).wait_recv()
        own = own + recv_buf[n_groups + outer].astype(jnp.float32)
    out_ref[...] = visit[0].astype(jnp.float32) - mie_ref[...] * own
    sent = direct()
    for hop in range(1, ahead + 1):
        sent += along(hop, source_ref) + across(hop)
    for copy in sent:
        copy.wait_send()
    for copy in started:
        copy.wait_send()


def solution(mesh):
    n_blk = mesh.shape["blk"]
    n_deg = mesh.shape["deg"]

    def local(source, operators, mie_factor, pair_source, pair_class, pair_scale):
        rows, spheres = source.shape
        classes, full, _ = operators.shape
        steps, slots, _ = pair_source.shape
        group = 2 if n_deg % 2 == 0 else 1
        main, tail = window_of(rows, full, n_deg)
        vmem = pl.BlockSpec(memory_space=pltpu.VMEM)
        return pl.pallas_call(
            functools.partial(kernel, n_blk, n_deg),
            out_shape=jax.ShapeDtypeStruct((rows, spheres), jnp.float32),
            in_specs=[pl.BlockSpec(memory_space=pltpu.HBM)] * 6,
            out_specs=vmem,
            scratch_shapes=[
                pltpu.VMEM((rows, spheres), jnp.float32),
                pltpu.VMEM(pair_source.shape, pair_source.dtype),
                pltpu.VMEM(pair_class.shape, pair_class.dtype),
                pltpu.VMEM(pair_scale.shape, pair_scale.dtype),
                pltpu.SemaphoreType.DMA((5,)),
                pltpu.VMEM((steps, rows, spheres), jnp.bfloat16),
                pltpu.VMEM((slots, spheres // 16, 16, spheres), jnp.bfloat16),
                pltpu.VMEM((classes, main + tail, spheres), jnp.float32),
                pltpu.VMEM((n_deg, classes, rows, full), jnp.bfloat16),
                pltpu.VMEM((2 * (n_deg // group), rows, spheres), jnp.bfloat16),
                pltpu.VMEM((2 * (n_deg // group), rows, spheres), jnp.bfloat16),
                pltpu.SemaphoreType.DMA((2 * ((steps - 1) // 2) + 1, pieces_of(rows))),
                pltpu.SemaphoreType.DMA((steps, pieces_of(rows))),
                pltpu.SemaphoreType.DMA((2 * (n_deg // group),)),
                pltpu.SemaphoreType.DMA((2 * (n_deg // group),)),
                pltpu.SemaphoreType.DMA((n_deg,)),
            ],
            compiler_params=pltpu.CompilerParams(
                collective_id=0, has_side_effects=True, vmem_limit_bytes=56 * 1024 * 1024
            ),
        )(source, operators, mie_factor, pair_source, pair_class, pair_scale)

    return jax.shard_map(
        local,
        mesh=mesh,
        in_specs=(
            P("deg", "blk"),
            P(),
            P("deg", "blk"),
            P(None, None, "blk"),
            P(None, None, "blk"),
            P(None, None, "blk"),
        ),
        out_specs=P("deg", "blk"),
        check_vma=False,
    )
```
